128 devices in a mesh: row: 8 (over x, z_hi), col: 16 (over z_lo, y, core).
Axes of the slice: x: 4, y: 4, z: 4 (z_hi: 2, z_lo: 2; z = z_hi * 2 + z_lo), core: 2. Of those that a mesh axis runs over, the one named last changes fastest.
Arguments:
- contact_map: bfloat16 [1024, 1024, 128], P('row', 'col'), may hold values from -6 to 6
- kernel_near: bfloat16 [3, 3, 128, 128], replicated, may hold values from -0.25 to 0.25
- offset_near: float32 [128], replicated, may hold values from -3 to 3
- kernel_mid: bfloat16 [3, 3, 128, 128], replicated, may hold values from -0.25 to 0.25
- offset_mid: float32 [128], replicated, may hold values from -3 to 3
- kernel_far: bfloat16 [3, 3, 128, 128], replicated, may hold values from -0.25 to 0.25
- offset_far: float32 [128], replicated, may hold values from -3 to 3
Outputs:
- refined: bfloat16 [1024, 1024, 128], P('row', 'col')
The draws below stay inside these ranges and needn't reach their ends.
All inputs are finite; a program needn't handle non-finite values.
Results may differ from the reference program's by a relative error of at most 0.013.
Values may be sent and summed in bfloat16 or wider, within the bound.
A program may use at most 64 MiB of HBM per device.

```python
import jax
import jax.numpy as jnp
from jax import lax

CH = 128
NBINS = 1024


def shard_levels(own_key, dims, shards, least, largest):
    gain, own = 1.0, jax.random.fold_in(own_key, 6)
    for axis_at, shards_of in shards:
        steps = jnp.exp(jax.random.uniform(jax.random.fold_in(own, axis_at), (shards_of,), jnp.float32, least / len(shards), largest / len(shards)))
        gain = gain * jnp.repeat(steps, dims[axis_at] // shards_of).reshape([-1 if axis == axis_at else 1 for axis in range(len(dims))])
    return gain


def centred(rng, extent, width, bound, split=(), held_as=jnp.bfloat16):
    values = width * jax.random.normal(rng, extent, jnp.float32)
    if split:
        values = values * shard_levels(rng, extent, split, -0.22, 0.18)
    return jnp.clip(values, -bound, bound).astype(held_as)


def setup_inputs(seed: int = 0) -> dict:
    keys = jax.random.split(jax.random.key(seed), 8)
    return {
        "contact_map": centred(keys[0], (NBINS, NBINS, CH), 1.0, 6.0, ((0, 8), (1, 16))),
        "kernel_near": centred(keys[1], (3, 3, CH, CH), (9 * CH // 2) ** -0.5, 0.25),
        "offset_near": centred(keys[2], (CH,), 0.5, 3.0, (), jnp.float32),
        "kernel_mid": centred(keys[3], (3, 3, CH, CH), (9 * CH // 2) ** -0.5, 0.25),
        "offset_mid": centred(keys[4], (CH,), 0.5, 3.0, (), jnp.float32),
        "kernel_far": centred(keys[5], (3, 3, CH, CH), (9 * CH // 2) ** -0.5, 0.25),
        "offset_far": centred(keys[6], (CH,), 0.5, 3.0, (), jnp.float32),
    }


def convolve(field, kernel, offset, dilation):
    result = lax.conv_general_dilated(field.astype(jnp.float32)[None], kernel.astype(jnp.float32), (1, 1), ((dilation, dilation), (dilation, dilation)), rhs_dilation=(dilation, dilation), dimension_numbers=("NHWC", "HWIO", "NHWC"), precision=lax.Precision.HIGHEST)[0]
    return result + offset


def reference(contact_map, kernel_near, offset_near, kernel_mid, offset_mid, kernel_far, offset_far):
    layer_one = jnp.maximum(convolve(contact_map, kernel_near, offset_near, 1), 0.0).astype(jnp.bfloat16)
    layer_two = jnp.maximum(convolve(layer_one, kernel_mid, offset_mid, 2), 0.0).astype(jnp.bfloat16)
    flipped = jnp.swapaxes(layer_two, 0, 1)
    averaged = ((layer_two.astype(jnp.float32) + flipped.astype(jnp.float32)) * 0.5).astype(jnp.bfloat16)
    return convolve(averaged, kernel_far, offset_far, 4).astype(jnp.bfloat16)
```

```python
import jax
import jax.numpy as jnp
from jax import lax
from jax.experimental import pallas as pl
from jax.experimental.pallas import tpu as pltpu
from jax.sharding import PartitionSpec as P

MESH = pl.DeviceIdType.MESH
F32, BF16 = jnp.float32, jnp.bfloat16

FLIPS = {
    "x0": ((1, 0, 0), 2),
    "x1": ((3, 0, 0), 6),
    "y0": ((0, 1, 0), 1),
    "y1": ((0, 3, 0), 3),
    "z0": ((0, 0, 1), 4),
    "z1": ((0, 0, 3), 5),
}
PATHS = {
    1: ("y0z1 z0", "z0z1 y0"),
    2: ("y1 x0y0", "y0y1 x0"),
    3: ("x0z1 y1z0", "z0z1 x0y1"),
    4: ("x1z0 x0", "x0x1z0"),
    5: ("x1z1 y0 x0", "x0y0z1 x1"),
    6: ("y1 y0z0 x1", "z0 x1y0y1"),
    7: ("x1y1z1", "y1z1 x1"),
}
STEPS = 8
ROWS = 16
LAG = (2, 2, 4)
SLOTS = len(LAG)


def segment(text):
    flips, change = [0, 0, 0], 0
    for at in range(0, len(text), 2):
        move, turn = FLIPS[text[at : at + 2]]
        flips = [a ^ b for a, b in zip(flips, move)]
        change ^= turn
    return tuple(flips), change


def plan():
    hops = []
    for start, paths in PATHS.items():
        for path, text in enumerate(paths):
            here, came = start, None
            for depth, part in enumerate(text.split()):
                flips, change = segment(part)
                hops.append([start, path, depth, here, flips, came])
                here, came = here ^ change, flips
            hops.append([start, path, depth + 1, here, None, came])
    relays = {w: [] for w in range(8)}
    for start, path, depth, here, flips, came in hops:
        if depth and flips is not None:
            relays[here].append((depth, start, path))
    slot = {}
    for w, held in relays.items():
        held.sort()
        taken = set()
        for depth, start, path in held:
            options = (2,) if depth == 2 else (0, 1, 2)
            at = [s for s in options if s not in taken][0]
            taken.add(at)
            slot[start, path, depth] = at
    out = [[0] * 8 for _ in range(2 + SLOTS)]
    into = [[0] * 8 for _ in range(2 + SLOTS)]
    code = lambda f: f[0] + 4 * f[1] + 16 * f[2]
    for start, path, depth, here, flips, came in hops:
        own = path if depth == 0 else None if flips is None else 2 + slot[start, path, depth]
        if flips is not None:
            after = slot.get((start, path, depth + 1))
            final = after is None
            out[own][here] = code(flips) + 64 * final + 128 * (path if final else after) + 512
        if came is not None:
            into[path if flips is None else own][here] = code(came) + 512
    return out, into


OUT, INTO = plan()


def pick(w, values):
    result = jnp.int32(values[0])
    for k in range(1, 8):
        result = jnp.where(w == k, jnp.int32(values[k]), result)
    return result


def both(a, b):
    return jnp.logical_and(a, b)


def flipped(value, by):
    return ((value // 2 + by // 2) % 2) * 2 + (value + by) % 2


ALL, LEFT, RIGHT = slice(0, 64), slice(0, 8), slice(56, 64)
HALO = []
for lo, hi in ((0, 32), (32, 128)):
    HALO.append((0, -1, slice(lo, hi), LEFT, "r", slice(8 + lo, 8 + hi)))
    HALO.append((0, 1, slice(lo, hi), RIGHT, "l", slice(8 + lo, 8 + hi)))
for di, src, dst in ((1, slice(120, 128), slice(0, 8)), (-1, slice(0, 8), slice(136, 144))):
    HALO.append((di, 0, src, ALL, "c", dst))
    HALO.append((di, -1, src, LEFT, "r", dst))
    HALO.append((di, 1, src, RIGHT, "l", dst))


def kernel(
    x, k1, b1, k2, b2, k3, b3, out,
    xc, xl, xr, x3, l1, l2, direct, turned, inside, w1, w2, w3, bufs, result,
    load_sem, halo_send, halo_recv, send_sem, recv_sem, out_sem,
):
    i, j = lax.axis_index("row"), lax.axis_index("col")
    cx, cy, cz, core = i // 2, (j // 2) % 4, (i % 2) * 2 + j // 8, j % 2
    u1 = (cx // 2 + cz) % 2
    u2 = (cx + cy // 2) % 2
    u3 = (cy + cz // 2) % 2
    w = u1 * 4 + u2 * 2 + u3
    fixed = w == 0

    def chip(flips, c):
        x_ = flipped(cx, flips % 4)
        y_ = flipped(cy, (flips // 4) % 4)
        z_ = flipped(cz, (flips // 16) % 4)
        return (x_ * 2 + z_ // 2, (z_ % 2) * 8 + y_ * 2 + c)

    loads = [(x, xc.at[8:136])]
    for k, wide in ((k1, w1), (k2, w2)):
        loads.append((k, wide.at[0:1152, 0:128]))
        loads.append((k, wide.at[384:1536, 128:256]))
    loads.append((k3, w3.at[:, 0:128]))
    for a in range(3):
        for e in range(3):
            loads.append(
                (k3.at[pl.ds((e * 3 + a) * 128, 128)], w3.at[pl.ds((a * 3 + e) * 128, 128), 128:256])
            )
    loads = [pltpu.make_async_copy(s, d, load_sem.at[n]) for n, (s, d) in enumerate(loads)]
    for copy in loads:
        copy.start()

    barrier = pltpu.get_barrier_semaphore()
    out_codes = [pick(w, v) for v in OUT]
    in_codes = [pick(w, v) for v in INTO]

    def greet(device):
        pl.semaphore_signal(barrier, 1, device_id=device, device_id_type=MESH)

    def exists(di, dj):
        ok = None
        for ok_ in ([i + di >= 0, i + di < 8] if di else []) + ([j + dj >= 0, j + dj < 16] if dj else []):
            ok = ok_ if ok is None else both(ok, ok_)
        return ok

    expected = jnp.int32(0)
    for di in (-1, 0, 1):
        for dj in (-1, 0, 1):
            if di or dj:
                ok = exists(di, dj)
                expected = expected + jnp.where(ok, 1, 0)
                pl.when(ok)(lambda di=di, dj=dj: greet((i + di, j + dj)))

    @pl.when(fixed)
    def _():
        greet((i, j + 1 - 2 * core))

    expected = expected + jnp.where(fixed, 1, 0)
    for n in range(2 + SLOTS):
        came, goes = in_codes[n], out_codes[n]

        @pl.when(came >= 512)
        def _():
            if n < 2:
                greet(chip(came, 0))
                greet(chip(came, 1))
            else:
                greet(chip(came, core))

        expected = expected + jnp.where(goes >= 512, 1 + (goes // 64) % 2, 0)
    pl.semaphore_wait(barrier, expected)

    targets = {"c": xc, "l": xl, "r": xr}
    halo = []
    for n, (di, dj, rows, cols, name, into) in enumerate(HALO):
        copy = pltpu.make_async_remote_copy(
            x.at[rows, cols],
            targets[name].at[into],
            halo_send.at[n],
            halo_recv.at[n],
            device_id=(i + di, j + dj),
            device_id_type=MESH,
        )
        goes, comes = exists(di, dj), exists(-di, -dj)
        halo.append((copy, goes, comes))
        pl.when(goes)(copy.start)

        @pl.when(jnp.logical_not(comes))
        def _():
            ref = targets[name].at[into]
            ref[...] = jnp.zeros(ref.shape, BF16)

    for wide in (w1, w2):
        wide[1152:1536, 0:128] = jnp.zeros((384, 128), BF16)
        wide[0:384, 128:256] = jnp.zeros((384, 128), BF16)
    column = lax.broadcasted_iota(jnp.int32, (80, 128), 0) + (j * 64 - 8)
    inside[...] = jnp.where(both(column >= 0, column < 1024), 1.0, 0.0).astype(F32)
    for copy in loads:
        copy.wait()

    def halo_wait(ns):
        for n in ns:
            copy, _, comes = halo[n]
            pl.when(comes)(copy.wait_recv)

    def spread(row):
        v = jnp.concatenate([xl[row].astype(F32), xc[row].astype(F32), xr[row].astype(F32)], axis=0)
        x3[row, :, 0:128] = pltpu.roll(v, 1, 0).astype(BF16)
        x3[row, :, 128:256] = v.astype(BF16)
        x3[row, :, 256:384] = pltpu.roll(v, 79, 0).astype(BF16)

    def pair_conv(ref, wide, bias, rows, d):
        lhs = jnp.concatenate(
            [jnp.concatenate([ref[r + (n - 1) * d] for n in range(4)], axis=-1) for r in rows], axis=0
        )
        total = jnp.dot(lhs, wide[...], preferred_element_type=F32)
        keep = inside[...]
        done = []
        for n, r in enumerate(rows):
            for m in range(2):
                v = total[n * 80 : n * 80 + 80, m * 128 : m * 128 + 128]
                done.append((r + m * d, jnp.maximum(v + bias[...], 0.0) * keep))
        return done

    def near(base, count):
        for row, v in pair_conv(x3, w1, b1, [base + 2 * n for n in range(count // 2)], 1):
            l1[row, :, 0:128] = pltpu.roll(v, 2, 0).astype(BF16)
            l1[row, :, 128:256] = v.astype(BF16)
            l1[row, :, 256:384] = pltpu.roll(v, 78, 0).astype(BF16)

    def middle(base, count):
        rows = [base + 4 * n + s for n in range(count // 4) for s in range(2)]
        for row, v in pair_conv(l1, w2, b2, rows, 2):
            l2[row, :, 0:128] = pltpu.roll(v, 4, 0)[8:72].astype(BF16)
            l2[row, :, 128:256] = v[8:72].astype(BF16)
            l2[row, :, 256:384] = pltpu.roll(v, 76, 0)[8:72].astype(BF16)

    def far(t):
        base = t * ROWS
        lhs = jnp.concatenate(
            [jnp.concatenate([l2[base + 8 + r + 4 * a] for a in (-1, 0, 1)], axis=-1) for r in range(ROWS)], axis=0
        )
        total = jnp.dot(lhs, w3[...], preferred_element_type=F32)
        for r in range(ROWS):
            direct[base + r] = total[r * 64 : r * 64 + 64, 0:128] * 0.5 + b3[...]
            turned[pl.ds(r, 64, stride=ROWS), :] = total[r * 64 : r * 64 + 64, 128:256] * 0.5
        for path in range(2):
            v = turned[path * 512 : path * 512 + 512, :]
            bufs[7 + path, t] = v.reshape(32, ROWS, 128).astype(BF16)

    def hop(n, t):
        code = out_codes[n]
        final = (code // 64) % 2
        which = (code // 128) % 4
        c = jnp.where(final == 1, t // 4, core)
        slot = jnp.where(final == 1, core * 2 + which, 4 + which)
        return pltpu.make_async_remote_copy(
            bufs.at[7 + n if n < 2 else 2 + n, t],
            bufs.at[slot, t],
            send_sem.at[n, t],
            recv_sem.at[slot, t],
            device_id=chip(code, c),
            device_id_type=MESH,
        )

    def across(n, t):
        return pltpu.make_async_remote_copy(
            bufs.at[7 + n, t],
            bufs.at[core * 2 + n, t],
            send_sem.at[n, t],
            recv_sem.at[core * 2 + n, t],
            device_id=(i, j + 1 - 2 * core),
            device_id_type=MESH,
        )

    def arrived(slot, t):
        pltpu.make_async_copy(bufs.at[slot, t], bufs.at[slot, t], recv_sem.at[slot, t]).wait()

    def send(t):
        for n in range(2):
            pl.when(jnp.logical_not(fixed))(lambda n=n: hop(n, t).start())
            pl.when(both(fixed, t // 4 != core))(lambda n=n: across(n, t).start())

            @pl.when(both(fixed, t // 4 == core))
            def _():
                pltpu.make_async_copy(
                    bufs.at[7 + n, t], bufs.at[core * 2 + n, t], recv_sem.at[core * 2 + n, t]
                ).start()

    def relay(s, t):
        @pl.when(out_codes[2 + s] >= 512)
        def _():
            arrived(4 + s, t)
            hop(2 + s, t).start()

    halo_wait([0, 1, 4, 5, 6])
    for row in range(1, 15):
        spread(row)
    near(2, 12)

    @pl.when(i == 0)
    def _():
        l1[2:8] = jnp.zeros((6, 80, 384), BF16)

    middle(4, 8)

    @pl.when(i == 0)
    def _():
        l2[4:8] = jnp.zeros((4, 64, 384), BF16)

    def step(t, carry):
        @pl.when(t == 1)
        def _():
            halo_wait([2, 3])

        @pl.when(t == 7)
        def _():
            halo_wait([7, 8, 9])

        base = t * ROWS
        for r in range(ROWS):
            spread(base + 15 + r)
        near(base + 14, ROWS)

        @pl.when(both(i == 7, t == 7))
        def _():
            l1[136:142] = jnp.zeros((6, 80, 384), BF16)

        middle(base + 12, ROWS)

        @pl.when(both(i == 7, t == 7))
        def _():
            l2[136:140] = jnp.zeros((4, 64, 384), BF16)

        far(t)
        send(t)
        for s in range(SLOTS):
            pl.when(t >= LAG[s])(lambda s=s: relay(s, t - LAG[s]))
        return carry

    lax.fori_loop(0, STEPS, step, 0)

    stores = []
    for late in range(6):
        for s in range(SLOTS):
            if late < LAG[s]:
                relay(s, STEPS + late - LAG[s])
        m = late - 2
        if m >= 0:
            t = core * 4 + m
            cols = slice(m * ROWS, m * ROWS + ROWS)
            for q in range(2):
                for path in range(2):
                    slot = q * 2 + path
                    arrived(slot, t)
                    rows = slice(slot * 32, slot * 32 + 32)
                    total = direct[rows, cols] + bufs[slot, t].astype(F32)
                    result[rows, cols] = total.astype(BF16)
            store = pltpu.make_async_copy(result.at[:, cols], out.at[:, cols], out_sem.at[m])
            store.start()
            stores.append(store)

    for copy, goes, _ in halo:
        pl.when(goes)(copy.wait_send)
    for t in range(STEPS):
        for n in range(2 + SLOTS):
            pl.when(out_codes[n] >= 512)(lambda n=n: hop(n, t).wait_send())
        for n in range(2):
            pl.when(both(fixed, t // 4 != core))(lambda n=n: across(n, t).wait_send())
    for store in stores:
        store.wait()


def local(contact_map, kernel_near, offset_near, kernel_mid, offset_mid, kernel_far, offset_far):
    anywhere, vmem = pl.BlockSpec(memory_space=pl.ANY), pl.BlockSpec(memory_space=pltpu.VMEM)
    args = [contact_map]
    for k, b in ((kernel_near, offset_near), (kernel_mid, offset_mid), (kernel_far, offset_far)):
        args += [k.reshape(9 * 128, 128), b.reshape(1, 128)]
    dma = pltpu.SemaphoreType.DMA
    return pl.pallas_call(
        kernel,
        out_shape=jax.ShapeDtypeStruct((128, 64, 128), BF16),
        in_specs=[anywhere] + [anywhere, vmem] * 3,
        out_specs=anywhere,
        scratch_shapes=[
            pltpu.VMEM((144, 64, 128), BF16),
            pltpu.VMEM((144, 8, 128), BF16),
            pltpu.VMEM((144, 8, 128), BF16),
            pltpu.VMEM((144, 80, 384), BF16),
            pltpu.VMEM((144, 80, 384), BF16),
            pltpu.VMEM((144, 64, 384), BF16),
            pltpu.VMEM((128, 64, 128), F32),
            pltpu.VMEM((1024, 128), F32),
            pltpu.VMEM((80, 128), F32),
            pltpu.VMEM((1536, 256), BF16),
            pltpu.VMEM((1536, 256), BF16),
            pltpu.VMEM((1152, 256), BF16),
            pltpu.VMEM((9, STEPS, 32, ROWS, 128), BF16),
            pltpu.VMEM((128, 64, 128), BF16),
            dma((15,)),
            dma((len(HALO),)),
            dma((len(HALO),)),
            dma((2 + SLOTS, STEPS)),
            dma((7, STEPS)),
            dma((4,)),
        ],
        compiler_params=pltpu.CompilerParams(
            collective_id=0, has_side_effects=True, vmem_limit_bytes=60 * 1024 * 1024
        ),
        name="trunk",
    )(*args)


def solution(mesh):
    in_specs = (P("row", "col", None), P(), P(), P(), P(), P(), P())
    return jax.shard_map(local, mesh=mesh, in_specs=in_specs, out_specs=P("row", "col", None), check_vma=False)
```

```python
import jax
import jax.numpy as jnp
from jax import lax
from jax.experimental import pallas as pl
from jax.experimental.pallas import tpu as pltpu
from jax.sharding import PartitionSpec as P

MESH = pl.DeviceIdType.MESH
F32, BF16 = jnp.float32, jnp.bfloat16

FLIPS = {
    "x0": ((1, 0, 0), 2),
    "x1": ((3, 0, 0), 6),
    "y0": ((0, 1, 0), 1),
    "y1": ((0, 3, 0), 3),
    "z0": ((0, 0, 1), 4),
    "z1": ((0, 0, 3), 5),
}
PATHS = {
    1: ("y0z1 z0", "z0z1 y0"),
    2: ("y1 x0y0", "y0y1 x0"),
    3: ("x0z1 y1z0", "z0z1 x0y1"),
    4: ("x1z0 x0", "x0x1z0"),
    5: ("x1z1 y0 x0", "x0y0z1 x1"),
    6: ("y1 y0z0 x1", "z0 x1y0y1"),
    7: ("x1y1z1", "y1z1 x1"),
}
STEPS = 16
ROWS = 8
LAG = (3, 3, 6)
SLOTS = len(LAG)
HALF = STEPS // 2


def segment(text):
    flips, change = [0, 0, 0], 0
    for at in range(0, len(text), 2):
        move, turn = FLIPS[text[at : at + 2]]
        flips = [a ^ b for a, b in zip(flips, move)]
        change ^= turn
    return tuple(flips), change


def plan():
    hops = []
    for start, paths in PATHS.items():
        for path, text in enumerate(paths):
            here, came = start, None
            for depth, part in enumerate(text.split()):
                flips, change = segment(part)
                hops.append([start, path, depth, here, flips, came])
                here, came = here ^ change, flips
            hops.append([start, path, depth + 1, here, None, came])
    relays = {w: [] for w in range(8)}
    for start, path, depth, here, flips, came in hops:
        if depth and flips is not None:
            relays[here].append((depth, start, path))
    slot = {}
    for w, held in relays.items():
        held.sort()
        taken = set()
        for depth, start, path in held:
            options = (2,) if depth == 2 else (0, 1, 2)
            at = [s for s in options if s not in taken][0]
            taken.add(at)
            slot[start, path, depth] = at
    out = [[0] * 8 for _ in range(2 + SLOTS)]
    into = [[0] * 8 for _ in range(2 + SLOTS)]
    code = lambda f: f[0] + 4 * f[1] + 16 * f[2]
    for start, path, depth, here, flips, came in hops:
        own = path if depth == 0 else None if flips is None else 2 + slot[start, path, depth]
        if flips is not None:
            after = slot.get((start, path, depth + 1))
            final = after is None
            out[own][here] = code(flips) + 64 * final + 128 * (path if final else after) + 512
        if came is not None:
            into[path if flips is None else own][here] = code(came) + 512
    return out, into


OUT, INTO = plan()


def pick(w, values):
    result = jnp.int32(values[0])
    for k in range(1, 8):
        result = jnp.where(w == k, jnp.int32(values[k]), result)
    return result


def both(a, b):
    return jnp.logical_and(a, b)


def flipped(value, by):
    return ((value // 2 + by // 2) % 2) * 2 + (value + by) % 2


ALL, LEFT, RIGHT = slice(0, 64), slice(0, 8), slice(56, 64)
HALO = []
for lo, hi in ((0, 24), (24, 64), (64, 128)):
    HALO.append((0, -1, slice(lo, hi), LEFT, "r", slice(8 + lo, 8 + hi)))
    HALO.append((0, 1, slice(lo, hi), RIGHT, "l", slice(8 + lo, 8 + hi)))
for di, src, dst in ((1, slice(120, 128), slice(0, 8)), (-1, slice(0, 8), slice(136, 144))):
    HALO.append((di, 0, src, ALL, "c", dst))
    HALO.append((di, -1, src, LEFT, "r", dst))
    HALO.append((di, 1, src, RIGHT, "l", dst))


def kernel(
    x, k1, c1, k2, c2, k3, c3, out,
    xc, xl, xr, x3, l1, l2, direct, turned, inside, w1, w2, w3, b1, b2, b3, bufs,
    load_sem, halo_send, halo_recv, send_sem, recv_sem,
):
    i, j = lax.axis_index("row"), lax.axis_index("col")
    cx, cy, cz, core = i // 2, (j // 2) % 4, (i % 2) * 2 + j // 8, j % 2
    u1 = (cx // 2 + cz) % 2
    u2 = (cx + cy // 2) % 2
    u3 = (cy + cz // 2) % 2
    w = u1 * 4 + u2 * 2 + u3
    fixed = w == 0

    def chip(flips, c):
        x_ = flipped(cx, flips % 4)
        y_ = flipped(cy, (flips // 4) % 4)
        z_ = flipped(cz, (flips // 16) % 4)
        return (x_ * 2 + z_ // 2, (z_ % 2) * 8 + y_ * 2 + c)

    loads = [(x, xc.at[8:136]), (c1, b1), (c2, b2), (c3, b3)]
    for k, wide in ((k1, w1), (k2, w2)):
        loads.append((k, wide.at[0:1152, 0:128]))
        loads.append((k, wide.at[384:1536, 128:256]))
    loads.append((k3, w3.at[:, 0:128]))
    for a in range(3):
        for e in range(3):
            loads.append(
                (k3.at[pl.ds((e * 3 + a) * 128, 128)], w3.at[pl.ds((a * 3 + e) * 128, 128), 128:256])
            )
    loads = [pltpu.make_async_copy(s, d, load_sem.at[n]) for n, (s, d) in enumerate(loads)]
    for copy in loads:
        copy.start()

    barrier = pltpu.get_barrier_semaphore()
    out_codes = [pick(w, v) for v in OUT]
    in_codes = [pick(w, v) for v in INTO]

    def greet(device):
        pl.semaphore_signal(barrier, 1, device_id=device, device_id_type=MESH)

    def exists(di, dj):
        ok = None
        for ok_ in ([i + di >= 0, i + di < 8] if di else []) + ([j + dj >= 0, j + dj < 16] if dj else []):
            ok = ok_ if ok is None else both(ok, ok_)
        return ok

    expected = jnp.int32(0)
    for di in (-1, 0, 1):
        for dj in (-1, 0, 1):
            if di or dj:
                ok = exists(di, dj)
                expected = expected + jnp.where(ok, 1, 0)
                pl.when(ok)(lambda di=di, dj=dj: greet((i + di, j + dj)))

    @pl.when(fixed)
    def _():
        greet((i, j + 1 - 2 * core))

    expected = expected + jnp.where(fixed, 1, 0)
    for n in range(2 + SLOTS):
        came, goes = in_codes[n], out_codes[n]

        @pl.when(came >= 512)
        def _():
            if n < 2:
                greet(chip(came, 0))
                greet(chip(came, 1))
            else:
                greet(chip(came, core))

        expected = expected + jnp.where(goes >= 512, 1 + (goes // 64) % 2, 0)
    pl.semaphore_wait(barrier, expected)

    targets = {"c": xc, "l": xl, "r": xr}
    halo = []
    for n, (di, dj, rows, cols, name, into) in enumerate(HALO):
        copy = pltpu.make_async_remote_copy(
            x.at[rows, cols],
            targets[name].at[into],
            halo_send.at[n],
            halo_recv.at[n],
            device_id=(i + di, j + dj),
            device_id_type=MESH,
        )
        goes, comes = exists(di, dj), exists(-di, -dj)
        halo.append((copy, goes, comes))
        pl.when(goes)(copy.start)

        @pl.when(jnp.logical_not(comes))
        def _():
            ref = targets[name].at[into]
            ref[...] = jnp.zeros(ref.shape, BF16)

    for wide in (w1, w2):
        wide[1152:1536, 0:128] = jnp.zeros((384, 128), BF16)
        wide[0:384, 128:256] = jnp.zeros((384, 128), BF16)
    column = lax.broadcasted_iota(jnp.int32, (80, 128), 0) + (j * 64 - 8)
    inside[0] = jnp.zeros((80, 128), F32)
    inside[1] = jnp.where(both(column >= 0, column < 1024), 1.0, 0.0).astype(F32)

    def keep(row):
        at = i * 128 + row - 8
        return inside[jnp.where(both(at >= 0, at < 1024), 1, 0)]

    for copy in loads:
        copy.wait()

    def halo_wait(ns):
        for n in ns:
            copy, _, comes = halo[n]
            pl.when(comes)(copy.wait_recv)

    def spread(row):
        v = jnp.concatenate([xl[row].astype(F32), xc[row].astype(F32), xr[row].astype(F32)], axis=0)
        x3[row, :, 0:128] = pltpu.roll(v, 1, 0).astype(BF16)
        x3[row, :, 128:256] = v.astype(BF16)
        x3[row, :, 256:384] = pltpu.roll(v, 79, 0).astype(BF16)

    def pair_conv(ref, wide, bias, rows, d):
        lhs = jnp.concatenate(
            [jnp.concatenate([ref[r + (n - 1) * d] for n in range(4)], axis=-1) for r in rows], axis=0
        )
        total = jnp.dot(lhs, wide[...], preferred_element_type=F32)
        done = []
        for n, r in enumerate(rows):
            for m in range(2):
                v = total[n * 80 : n * 80 + 80, m * 128 : m * 128 + 128]
                done.append((r + m * d, jnp.maximum(v + bias[...], 0.0) * keep(r + m * d)))
        return done

    def near(base, count):
        for row, v in pair_conv(x3, w1, b1, [base + 2 * n for n in range(count // 2)], 1):
            l1[row, :, 0:128] = pltpu.roll(v, 2, 0).astype(BF16)
            l1[row, :, 128:256] = v.astype(BF16)
            l1[row, :, 256:384] = pltpu.roll(v, 78, 0).astype(BF16)

    def middle(base, count):
        rows = [base + 4 * n + s for n in range(count // 4) for s in range(2)]
        for row, v in pair_conv(l1, w2, b2, rows, 2):
            l2[row, :, 0:128] = pltpu.roll(v, 4, 0)[8:72].astype(BF16)
            l2[row, :, 128:256] = v[8:72].astype(BF16)
            l2[row, :, 256:384] = pltpu.roll(v, 76, 0)[8:72].astype(BF16)

    def far(t):
        base = t * ROWS
        lhs = jnp.concatenate(
            [jnp.concatenate([l2[base + 8 + r + 4 * a] for a in (-1, 0, 1)], axis=-1) for r in range(ROWS)], axis=0
        )
        total = jnp.dot(lhs, w3[...], preferred_element_type=F32)
        for r in range(ROWS):
            direct[base + r] = total[r * 64 : r * 64 + 64, 0:128] * 0.5 + b3[...]
            turned[pl.ds(r, 64, stride=ROWS), :] = total[r * 64 : r * 64 + 64, 128:256] * 0.5
        for path in range(2):
            v = turned[path * 32 * ROWS : (path + 1) * 32 * ROWS, :]
            bufs[7 + path, t] = v.reshape(32, ROWS, 128).astype(BF16)

    goes_on = [code >= 512 for code in out_codes]
    ends = [(code // 64) % 2 == 1 for code in out_codes]
    where = [chip(code, 0) for code in out_codes]
    slots = [
        jnp.where(end, core * 2 + (code // 128) % 4, 4 + (code // 128) % 4) for code, end in zip(out_codes, ends)
    ]

    def hop(n, t):
        c = jnp.where(ends[n], t // HALF, core)
        row, col = where[n]
        return pltpu.make_async_remote_copy(
            bufs.at[7 + n if n < 2 else 2 + n, t],
            bufs.at[slots[n], t],
            send_sem.at[n],
            recv_sem.at[slots[n], t],
            device_id=(row, col + c),
            device_id_type=MESH,
        )

    def across(n, t):
        return pltpu.make_async_remote_copy(
            bufs.at[7 + n, t],
            bufs.at[core * 2 + n, t],
            send_sem.at[n],
            recv_sem.at[core * 2 + n, t],
            device_id=(i, j + 1 - 2 * core),
            device_id_type=MESH,
        )

    def arrived(slot, t):
        here = bufs.at[slot, t]
        pltpu.make_async_copy(here, here, recv_sem.at[slot, t]).wait()

    def send(t):
        @pl.when(jnp.logical_not(fixed))
        def _():
            for n in range(2):
                hop(n, t).start()

        @pl.when(both(fixed, t // HALF != core))
        def _():
            for n in range(2):
                across(n, t).start()

        @pl.when(both(fixed, t // HALF == core))
        def _():
            for n in range(2):
                own = core * 2 + n
                pltpu.make_async_copy(bufs.at[7 + n, t], bufs.at[own, t], recv_sem.at[own, t]).start()

    def relay(s, n):
        @pl.when(both(goes_on[2 + s], both(n >= LAG[s], n < STEPS + LAG[s])))
        def _():
            t = lax.rem(n - LAG[s] + 1, STEPS)
            arrived(4 + s, t)
            hop(2 + s, t).start()

    halo_wait([0, 1])

    def step(n, carry):
        @pl.when(n == 1)
        def _():
            halo_wait([2, 3])

        @pl.when(n == 6)
        def _():
            halo_wait([4, 5])

        @pl.when(n == 14)
        def _():
            halo_wait([9, 10, 11])

        @pl.when(n == 15)
        def _():
            halo_wait([6, 7, 8])

        last = n == STEPS - 1
        base = (n + 1) * ROWS
        for r in range(ROWS):
            spread(jnp.where(last, 1, jnp.maximum(base + 15, 8)) + r)
        near(jnp.where(last, 2, base + 14), ROWS)

        @pl.when(n >= -1)
        def _():
            middle(jnp.where(last, 4, base + 12), ROWS)

        @pl.when(n >= 0)
        def _():
            t = lax.rem(n + 1, STEPS)
            far(t)
            send(t)
            for s in range(SLOTS):
                relay(s, n)

        return carry

    lax.fori_loop(-2, STEPS, step, 0)

    def drain(d, carry):
        for s in range(SLOTS):
            relay(s, STEPS + d)

        @pl.when(d >= 1)
        def _():
            m = jnp.where(core == 0, lax.rem(d, HALF), d - 1)
            t = core * HALF + m
            cols = pl.ds(pl.multiple_of(m * ROWS, ROWS), ROWS)
            for slot in range(4):
                arrived(slot, t)
                rows = slice(slot * 32, slot * 32 + 32)
                out[rows, cols] = (direct[rows, cols] + bufs[slot, t].astype(F32)).astype(BF16)

        return carry

    lax.fori_loop(0, HALF + 1, drain, 0)

    for copy, goes, _ in halo:
        pl.when(goes)(copy.wait_send)
    for n in range(2 + SLOTS):

        @pl.when(goes_on[n])
        def _():
            sent = bufs.at[7 + n if n < 2 else 2 + n]
            pltpu.make_async_copy(sent, sent, send_sem.at[n]).wait()

    @pl.when(fixed)
    def _():
        for n in range(2):
            sent = bufs.at[7 + n, 0:HALF]
            pltpu.make_async_copy(sent, sent, send_sem.at[n]).wait()


def local(contact_map, kernel_near, offset_near, kernel_mid, offset_mid, kernel_far, offset_far):
    hbm, vmem = pl.BlockSpec(memory_space=pltpu.HBM), pl.BlockSpec(memory_space=pltpu.VMEM)
    args = [contact_map]
    for k, b in ((kernel_near, offset_near), (kernel_mid, offset_mid), (kernel_far, offset_far)):
        args += [k.reshape(9 * 128, 128), b.reshape(1, 128)]
    args = [pltpu.with_memory_space_constraint(v, pltpu.HBM) for v in args]
    dma = pltpu.SemaphoreType.DMA
    return pl.pallas_call(
        kernel,
        out_shape=jax.ShapeDtypeStruct((128, 64, 128), BF16),
        in_specs=[hbm] * 7,
        out_specs=vmem,
        scratch_shapes=[
            pltpu.VMEM((144, 64, 128), BF16),
            pltpu.VMEM((144, 8, 128), BF16),
            pltpu.VMEM((144, 8, 128), BF16),
            pltpu.VMEM((144, 80, 384), BF16),
            pltpu.VMEM((144, 80, 384), BF16),
            pltpu.VMEM((144, 64, 384), BF16),
            pltpu.VMEM((128, 64, 128), F32),
            pltpu.VMEM((64 * ROWS, 128), F32),
            pltpu.VMEM((2, 80, 128), F32),
            pltpu.VMEM((1536, 256), BF16),
            pltpu.VMEM((1536, 256), BF16),
            pltpu.VMEM((1152, 256), BF16),
            pltpu.VMEM((1, 128), F32),
            pltpu.VMEM((1, 128), F32),
            pltpu.VMEM((1, 128), F32),
            pltpu.VMEM((9, STEPS, 32, ROWS, 128), BF16),
            dma((18,)),
            dma((len(HALO),)),
            dma((len(HALO),)),
            dma((2 + SLOTS,)),
            dma((7, STEPS)),
        ],
        compiler_params=pltpu.CompilerParams(
            collective_id=0, has_side_effects=True, vmem_limit_bytes=50 * 1024 * 1024
        ),
        name="trunk",
    )(*args)


def solution(mesh):
    in_specs = (P("row", "col", None), P(), P(), P(), P(), P(), P())
    return jax.shard_map(local, mesh=mesh, in_specs=in_specs, out_specs=P("row", "col", None), check_vma=False)
```

```python
import jax
import jax.numpy as jnp
from jax import lax
from jax.experimental import pallas as pl
from jax.experimental.pallas import tpu as pltpu
from jax.sharding import PartitionSpec as P

MESH = pl.DeviceIdType.MESH
F32, BF16 = jnp.float32, jnp.bfloat16

FLIPS = {
    "x0": ((1, 0, 0), 2),
    "x1": ((3, 0, 0), 6),
    "y0": ((0, 1, 0), 1),
    "y1": ((0, 3, 0), 3),
    "z0": ((0, 0, 1), 4),
    "z1": ((0, 0, 3), 5),
}
PATHS = {
    1: ("y0z1 z0", "z0z1 y0"),
    2: ("y1 x0y0", "y0y1 x0"),
    3: ("x0z1 y1z0", "z0z1 x0y1"),
    4: ("x1z0 x0", "x0x1z0"),
    5: ("x1z1 y0 x0", "x0y0z1 x1"),
    6: ("y1 y0z0 x1", "z0 x1y0y1"),
    7: ("x1y1z1", "y1z1 x1"),
}
STEPS = 16
ROWS = 8
LAG = (3, 3, 6)
AHEAD = 3
DIRECT = 2
SLOTS = len(LAG)
HALF = STEPS // 2


def segment(text):
    flips, change = [0, 0, 0], 0
    for at in range(0, len(text), 2):
        move, turn = FLIPS[text[at : at + 2]]
        flips = [a ^ b for a, b in zip(flips, move)]
        change ^= turn
    return tuple(flips), change


def plan():
    hops = []
    for start, paths in PATHS.items():
        for path, text in enumerate(paths):
            here, came = start, None
            for depth, part in enumerate(text.split()):
                flips, change = segment(part)
                hops.append([start, path, depth, here, flips, came])
                here, came = here ^ change, flips
            hops.append([start, path, depth + 1, here, None, came])
    relays = {w: [] for w in range(8)}
    for start, path, depth, here, flips, came in hops:
        if depth and flips is not None:
            relays[here].append((depth, start, path))
    slot = {}
    for w, held in relays.items():
        held.sort()
        taken = set()
        for depth, start, path in held:
            options = (2,) if depth == 2 else (0, 1, 2)
            at = [s for s in options if s not in taken][0]
            taken.add(at)
            slot[start, path, depth] = at
    out = [[0] * 8 for _ in range(2 + SLOTS)]
    into = [[0] * 8 for _ in range(2 + SLOTS)]
    code = lambda f: f[0] + 4 * f[1] + 16 * f[2]
    for start, path, depth, here, flips, came in hops:
        own = path if depth == 0 else None if flips is None else 2 + slot[start, path, depth]
        if flips is not None:
            after = slot.get((start, path, depth + 1))
            final = after is None
            out[own][here] = code(flips) + 64 * final + 128 * (path if final else after) + 512
        if came is not None:
            into[path if flips is None else own][here] = code(came) + 512
    return out, into


OUT, INTO = plan()
STRAIGHT = [0] * 8
for start, paths in PATHS.items():
    if len(paths[0].split()) == 3:
        flips, _ = segment(paths[0].replace(" ", ""))
        STRAIGHT[start] = flips[0] + 4 * flips[1] + 16 * flips[2] + 64


def pick(w, values):
    result = jnp.int32(values[0])
    for k in range(1, 8):
        result = jnp.where(w == k, jnp.int32(values[k]), result)
    return result


def both(a, b):
    return jnp.logical_and(a, b)


def flipped(value, by):
    return ((value // 2 + by // 2) % 2) * 2 + (value + by) % 2


ALL, LEFT, RIGHT = slice(0, 64), slice(0, 8), slice(56, 64)
HALO = []
for lo, hi in ((0, 24), (24, 64), (64, 128)):
    HALO.append((0, -1, slice(lo, hi), LEFT, "r", slice(8 + lo, 8 + hi)))
    HALO.append((0, 1, slice(lo, hi), RIGHT, "l", slice(8 + lo, 8 + hi)))
for di, src, dst in ((1, slice(120, 128), slice(0, 8)), (-1, slice(0, 8), slice(136, 144))):
    HALO.append((di, 0, src, ALL, "c", dst))
    HALO.append((di, -1, src, LEFT, "r", dst))
    HALO.append((di, 1, src, RIGHT, "l", dst))


def kernel(
    x, k1, c1, k2, c2, k3, c3, out,
    xc, xl, xr, x3, l1, l2, direct, turned, inside, w1, w2, w3, b1, b2, b3, bufs,
    load_sem, halo_send, halo_recv, send_sem, side_sem, recv_sem,
):
    i, j = lax.axis_index("row"), lax.axis_index("col")
    cx, cy, cz, core = i // 2, (j // 2) % 4, (i % 2) * 2 + j // 8, j % 2
    u1 = (cx // 2 + cz) % 2
    u2 = (cx + cy // 2) % 2
    u3 = (cy + cz // 2) % 2
    w = u1 * 4 + u2 * 2 + u3
    fixed = w == 0

    def chip(flips, c):
        x_ = flipped(cx, flips % 4)
        y_ = flipped(cy, (flips // 4) % 4)
        z_ = flipped(cz, (flips // 16) % 4)
        return (x_ * 2 + z_ // 2, (z_ % 2) * 8 + y_ * 2 + c)

    loads = [(x, xc.at[8:136]), (c1, b1), (c2, b2), (c3, b3)]
    for k, wide in ((k1, w1), (k2, w2)):
        loads.append((k, wide.at[0:1152, 0:128]))
        loads.append((k, wide.at[384:1536, 128:256]))
    loads.append((k3, w3.at[:, 0:128]))
    for a in range(3):
        for e in range(3):
            loads.append(
                (k3.at[pl.ds((e * 3 + a) * 128, 128)], w3.at[pl.ds((a * 3 + e) * 128, 128), 128:256])
            )
    loads = [pltpu.make_async_copy(s, d, load_sem.at[n]) for n, (s, d) in enumerate(loads)]
    for copy in loads:
        copy.start()

    barrier = pltpu.get_barrier_semaphore()
    out_codes = [pick(w, v) for v in OUT]
    in_codes = [pick(w, v) for v in INTO]

    def greet(device):
        pl.semaphore_signal(barrier, 1, device_id=device, device_id_type=MESH)

    def exists(di, dj):
        ok = None
        for ok_ in ([i + di >= 0, i + di < 8] if di else []) + ([j + dj >= 0, j + dj < 16] if dj else []):
            ok = ok_ if ok is None else both(ok, ok_)
        return ok

    expected = jnp.int32(0)
    for di in (-1, 0, 1):
        for dj in (-1, 0, 1):
            if di or dj:
                ok = exists(di, dj)
                expected = expected + jnp.where(ok, 1, 0)
                pl.when(ok)(lambda di=di, dj=dj: greet((i + di, j + dj)))

    @pl.when(fixed)
    def _():
        greet((i, j + 1 - 2 * core))

    straight = pick(w, STRAIGHT)
    long = straight >= 64

    @pl.when(long)
    def _():
        greet(chip(straight, 0))
        greet(chip(straight, 1))

    expected = expected + jnp.where(fixed, 1, 0) + jnp.where(long, 2, 0)
    for n in range(2 + SLOTS):
        came, goes = in_codes[n], out_codes[n]

        @pl.when(came >= 512)
        def _():
            if n < 2:
                greet(chip(came, 0))
                greet(chip(came, 1))
            else:
                greet(chip(came, core))

        expected = expected + jnp.where(goes >= 512, 1 + (goes // 64) % 2, 0)
    pl.semaphore_wait(barrier, expected)

    targets = {"c": xc, "l": xl, "r": xr}
    halo = []
    for n, (di, dj, rows, cols, name, into) in enumerate(HALO):
        copy = pltpu.make_async_remote_copy(
            x.at[rows, cols],
            targets[name].at[into],
            halo_send.at[n],
            halo_recv.at[n],
            device_id=(i + di, j + dj),
            device_id_type=MESH,
        )
        goes, comes = exists(di, dj), exists(-di, -dj)
        halo.append((copy, goes, comes))
        pl.when(goes)(copy.start)

        @pl.when(jnp.logical_not(comes))
        def _():
            ref = targets[name].at[into]
            ref[...] = jnp.zeros(ref.shape, BF16)

    for wide in (w1, w2):
        wide[1152:1536, 0:128] = jnp.zeros((384, 128), BF16)
        wide[0:384, 128:256] = jnp.zeros((384, 128), BF16)
    column = lax.broadcasted_iota(jnp.int32, (80, 128), 0) + (j * 64 - 8)
    inside[0] = jnp.zeros((80, 128), F32)
    inside[1] = jnp.where(both(column >= 0, column < 1024), 1.0, 0.0).astype(F32)

    def keep(row):
        at = i * 128 + row - 8
        return inside[jnp.where(both(at >= 0, at < 1024), 1, 0)]

    for copy in loads:
        copy.wait()

    def halo_wait(ns):
        for n in ns:
            copy, _, comes = halo[n]
            pl.when(comes)(copy.wait_recv)

    def spread(row):
        v = jnp.concatenate([xl[row].astype(F32), xc[row].astype(F32), xr[row].astype(F32)], axis=0)
        x3[row, :, 0:128] = pltpu.roll(v, 1, 0).astype(BF16)
        x3[row, :, 128:256] = v.astype(BF16)
        x3[row, :, 256:384] = pltpu.roll(v, 79, 0).astype(BF16)

    def pair_conv(ref, wide, bias, rows, d):
        lhs = jnp.concatenate(
            [jnp.concatenate([ref[r + (n - 1) * d] for n in range(4)], axis=-1) for r in rows], axis=0
        )
        total = jnp.dot(lhs, wide[...], preferred_element_type=F32)
        done = []
        for n, r in enumerate(rows):
            for m in range(2):
                v = total[n * 80 : n * 80 + 80, m * 128 : m * 128 + 128]
                done.append((r + m * d, jnp.maximum(v + bias[...], 0.0) * keep(r + m * d)))
        return done

    def near(base, count):
        for row, v in pair_conv(x3, w1, b1, [base + 2 * n for n in range(count // 2)], 1):
            l1[row, :, 0:128] = pltpu.roll(v, 2, 0).astype(BF16)
            l1[row, :, 128:256] = v.astype(BF16)
            l1[row, :, 256:384] = pltpu.roll(v, 78, 0).astype(BF16)

    def middle(base, count):
        rows = [base + 4 * n + s for n in range(count // 4) for s in range(2)]
        for row, v in pair_conv(l1, w2, b2, rows, 2):
            l2[row, :, 0:128] = pltpu.roll(v, 4, 0)[8:72].astype(BF16)
            l2[row, :, 128:256] = v[8:72].astype(BF16)
            l2[row, :, 256:384] = pltpu.roll(v, 76, 0)[8:72].astype(BF16)

    def far(t):
        base = t * ROWS
        lhs = jnp.concatenate(
            [jnp.concatenate([l2[base + 8 + r + 4 * a] for a in (-1, 0, 1)], axis=-1) for r in range(ROWS)], axis=0
        )
        total = jnp.dot(lhs, w3[...], preferred_element_type=F32)
        for r in range(ROWS):
            direct[base + r] = total[r * 64 : r * 64 + 64, 0:128] * 0.5 + b3[...]
            turned[pl.ds(r, 64, stride=ROWS), :] = total[r * 64 : r * 64 + 64, 128:256] * 0.5
        for path in range(2):
            v = turned[path * 32 * ROWS : (path + 1) * 32 * ROWS, :]
            bufs[7 + path, t] = v.reshape(32, ROWS, 128).astype(BF16)

    goes_on = [code >= 512 for code in out_codes]
    ends = [(code // 64) % 2 == 1 for code in out_codes]
    where = [chip(code, 0) for code in out_codes]
    slots = [
        jnp.where(end, core * 2 + (code // 128) % 4, 4 + (code // 128) % 4) for code, end in zip(out_codes, ends)
    ]

    target = chip(straight, 0)

    def hop(n, t, direct=None):
        row, col = where[n]
        end, slot = ends[n], slots[n]
        if direct is not None:
            row, col = jnp.where(direct, target[0], row), jnp.where(direct, target[1], col)
            end, slot = jnp.logical_or(direct, end), jnp.where(direct, core * 2, slot)
        return pltpu.make_async_remote_copy(
            bufs.at[7 + n if n < 2 else 2 + n, t],
            bufs.at[slot, t],
            send_sem.at[n, t],
            recv_sem.at[slot, t],
            device_id=(row, col + jnp.where(end, t // HALF, core)),
            device_id_type=MESH,
        )

    def across(n, t):
        return pltpu.make_async_remote_copy(
            bufs.at[7 + n, t],
            bufs.at[core * 2 + n, t],
            side_sem.at[n],
            recv_sem.at[core * 2 + n, t],
            device_id=(i, j + 1 - 2 * core),
            device_id_type=MESH,
        )

    def arrived(slot, t):
        here = bufs.at[slot, t]
        pltpu.make_async_copy(here, here, recv_sem.at[slot, t]).wait()

    def left(op, n):
        hop(op, lax.rem(n + 1, STEPS)).wait_send()

    def send(n):
        t = lax.rem(n + 1, STEPS)

        @pl.when(both(jnp.logical_not(fixed), n >= AHEAD))
        def _():
            for op in range(2):
                left(op, n - AHEAD)

        @pl.when(jnp.logical_not(fixed))
        def _():
            hop(0, t, both(long, n >= STEPS - DIRECT)).start()
            hop(1, t).start()

        @pl.when(both(fixed, t // HALF != core))
        def _():
            for n in range(2):
                across(n, t).start()

        @pl.when(both(fixed, t // HALF == core))
        def _():
            for n in range(2):
                own = core * 2 + n
                pltpu.make_async_copy(bufs.at[7 + n, t], bufs.at[own, t], recv_sem.at[own, t]).start()

    steps = [
        jnp.int32(STEPS - DIRECT) if s == 2 else jnp.where(ends[2 + s], STEPS, STEPS - DIRECT) for s in range(SLOTS)
    ]

    def relay(s, n):
        @pl.when(both(goes_on[2 + s], both(n >= LAG[s], n < steps[s] + LAG[s])))
        def _():
            t = lax.rem(n - LAG[s] + 1, STEPS)
            arrived(4 + s, t)
            pl.when(n >= LAG[s] + AHEAD)(lambda: left(2 + s, n - LAG[s] - AHEAD))
            hop(2 + s, t).start()

    def first(n, low, offset):
        return jnp.where(n >= STEPS - 1, low, (n + 1) * ROWS + offset)

    def feed(n):
        base = jnp.maximum(first(n, 1, 15), jnp.where(n < 0, 8, 0))
        for r in range(ROWS):
            spread(base + r)

    def one(n):
        near(first(n, 2, 14), ROWS)

    def two(n):
        middle(first(n, 4, 12), ROWS)

    halo_wait([0, 1])
    feed(jnp.int32(-2))

    def fill(n, carry):
        @pl.when(n == 0)
        def _():
            halo_wait([2, 3])

        one(n)
        feed(n + 1)
        pl.when(n >= -1)(lambda: two(n))
        return carry

    lax.fori_loop(-2, 1, fill, 0)

    def step(n, carry):
        for at, which in ((4, [4, 5]), (12, [9, 10, 11]), (13, [6, 7, 8])):
            pl.when(n == at)(lambda which=which: halo_wait(which))
        t = lax.rem(n + 1, STEPS)
        far(t)
        one(n + 1)
        feed(n + 2)
        send(n)
        relay(2, n)
        pl.when(n >= 0)(lambda: two(n + 1))
        relay(0, n)
        relay(1, n)
        return carry

    lax.fori_loop(0, STEPS, step, 0)

    def drain(d, carry):
        for s in range(SLOTS):
            relay(s, STEPS + d)

        @pl.when(d >= 1)
        def _():
            m = jnp.where(core == 0, lax.rem(d, HALF), d - 1)
            t = core * HALF + m
            cols = pl.ds(pl.multiple_of(m * ROWS, ROWS), ROWS)
            for slot in range(4):
                arrived(slot, t)
                rows = slice(slot * 32, slot * 32 + 32)
                out[rows, cols] = (direct[rows, cols] + bufs[slot, t].astype(F32)).astype(BF16)

        return carry

    lax.fori_loop(0, HALF + 1, drain, 0)

    for copy, goes, _ in halo:
        pl.when(goes)(copy.wait_send)
    for op in range(2 + SLOTS):

        @pl.when(goes_on[op])
        def _():
            for n in range(AHEAD):
                left(op, (STEPS if op < 2 else steps[op - 2]) - AHEAD + n)

    @pl.when(fixed)
    def _():
        for n in range(2):
            sent = bufs.at[7 + n, 0:HALF]
            pltpu.make_async_copy(sent, sent, side_sem.at[n]).wait()


def local(contact_map, kernel_near, offset_near, kernel_mid, offset_mid, kernel_far, offset_far):
    hbm, vmem = pl.BlockSpec(memory_space=pltpu.HBM), pl.BlockSpec(memory_space=pltpu.VMEM)
    args = [contact_map]
    for k, b in ((kernel_near, offset_near), (kernel_mid, offset_mid), (kernel_far, offset_far)):
        args += [k.reshape(9 * 128, 128), b.reshape(1, 128)]
    args = [pltpu.with_memory_space_constraint(v, pltpu.HBM) for v in args]
    dma = pltpu.SemaphoreType.DMA
    return pl.pallas_call(
        kernel,
        out_shape=jax.ShapeDtypeStruct((128, 64, 128), BF16),
        in_specs=[hbm] * 7,
        out_specs=vmem,
        scratch_shapes=[
            pltpu.VMEM((144, 64, 128), BF16),
            pltpu.VMEM((144, 8, 128), BF16),
            pltpu.VMEM((144, 8, 128), BF16),
            pltpu.VMEM((144, 80, 384), BF16),
            pltpu.VMEM((144, 80, 384), BF16),
            pltpu.VMEM((144, 64, 384), BF16),
            pltpu.VMEM((128, 64, 128), F32),
            pltpu.VMEM((64 * ROWS, 128), F32),
            pltpu.VMEM((2, 80, 128), F32),
            pltpu.VMEM((1536, 256), BF16),
            pltpu.VMEM((1536, 256), BF16),
            pltpu.VMEM((1152, 256), BF16),
            pltpu.VMEM((1, 128), F32),
            pltpu.VMEM((1, 128), F32),
            pltpu.VMEM((1, 128), F32),
            pltpu.VMEM((9, STEPS, 32, ROWS, 128), BF16),
            dma((18,)),
            dma((len(HALO),)),
            dma((len(HALO),)),
            dma((2 + SLOTS, STEPS)),
            dma((2,)),
            dma((7, STEPS)),
        ],
        compiler_params=pltpu.CompilerParams(
            collective_id=0, has_side_effects=True, vmem_limit_bytes=50 * 1024 * 1024
        ),
        name="trunk",
    )(*args)


def solution(mesh):
    in_specs = (P("row", "col", None), P(), P(), P(), P(), P(), P())
    return jax.shard_map(local, mesh=mesh, in_specs=in_specs, out_specs=P("row", "col", None), check_vma=False)
```

```python
import jax
import jax.numpy as jnp
from jax import lax
from jax.experimental import pallas as pl
from jax.experimental.pallas import tpu as pltpu
from jax.sharding import PartitionSpec as P

MESH = pl.DeviceIdType.MESH
F32, BF16 = jnp.float32, jnp.bfloat16

FLIPS = {
    "x0": ((1, 0, 0), 2),
    "x1": ((3, 0, 0), 6),
    "y0": ((0, 1, 0), 1),
    "y1": ((0, 3, 0), 3),
    "z0": ((0, 0, 1), 4),
    "z1": ((0, 0, 3), 5),
}
PATHS = {
    1: ("y0z1 z0", "z0z1 y0"),
    2: ("y1 x0y0", "y0y1 x0"),
    3: ("x0z1 y1z0", "z0z1 x0y1"),
    4: ("x1z0 x0", "x0x1z0"),
    5: ("x1z1 y0 x0", "x0y0z1 x1"),
    6: ("y1 y0z0 x1", "z0 x1y0y1"),
    7: ("x1y1z1", "y1z1 x1"),
}
STEPS = 16
ROWS = 8
LAG = (3, 3, 6)
AHEAD = 3
DIRECT = 2
SLOTS = len(LAG)
HALF = STEPS // 2


def segment(text):
    flips, change = [0, 0, 0], 0
    for at in range(0, len(text), 2):
        move, turn = FLIPS[text[at : at + 2]]
        flips = [a ^ b for a, b in zip(flips, move)]
        change ^= turn
    return tuple(flips), change


def plan():
    hops = []
    for start, paths in PATHS.items():
        for path, text in enumerate(paths):
            here, came = start, None
            for depth, part in enumerate(text.split()):
                flips, change = segment(part)
                hops.append([start, path, depth, here, flips, came])
                here, came = here ^ change, flips
            hops.append([start, path, depth + 1, here, None, came])
    relays = {w: [] for w in range(8)}
    for start, path, depth, here, flips, came in hops:
        if depth and flips is not None:
            relays[here].append((depth, start, path))
    slot = {}
    for w, held in relays.items():
        held.sort()
        taken = set()
        for depth, start, path in held:
            options = (2,) if depth == 2 else (0, 1, 2)
            at = [s for s in options if s not in taken][0]
            taken.add(at)
            slot[start, path, depth] = at
    out = [[0] * 8 for _ in range(2 + SLOTS)]
    into = [[0] * 8 for _ in range(2 + SLOTS)]
    code = lambda f: f[0] + 4 * f[1] + 16 * f[2]
    for start, path, depth, here, flips, came in hops:
        own = path if depth == 0 else None if flips is None else 2 + slot[start, path, depth]
        if flips is not None:
            after = slot.get((start, path, depth + 1))
            final = after is None
            out[own][here] = code(flips) + 64 * final + 128 * (path if final else after) + 512
        if came is not None:
            into[path if flips is None else own][here] = code(came) + 512
    return out, into


OUT, INTO = plan()
STRAIGHT = [0] * 8
for start, paths in PATHS.items():
    if len(paths[0].split()) == 3:
        flips, _ = segment(paths[0].replace(" ", ""))
        STRAIGHT[start] = flips[0] + 4 * flips[1] + 16 * flips[2] + 64


def pick(w, values):
    result = jnp.int32(values[0])
    for k in range(1, 8):
        result = jnp.where(w == k, jnp.int32(values[k]), result)
    return result


def both(a, b):
    return jnp.logical_and(a, b)


def flipped(value, by):
    return ((value // 2 + by // 2) % 2) * 2 + (value + by) % 2


ALL, LEFT, RIGHT = slice(0, 64), slice(0, 8), slice(56, 64)
HALO = []
for lo, hi in ((0, 24), (24, 64), (64, 128)):
    HALO.append((0, -1, slice(lo, hi), LEFT, "r", slice(8 + lo, 8 + hi)))
    HALO.append((0, 1, slice(lo, hi), RIGHT, "l", slice(8 + lo, 8 + hi)))
for di, src, dst in ((1, slice(120, 128), slice(0, 8)), (-1, slice(0, 8), slice(136, 144))):
    HALO.append((di, 0, src, ALL, "c", dst))
    HALO.append((di, -1, src, LEFT, "r", dst))
    HALO.append((di, 1, src, RIGHT, "l", dst))


def kernel(
    x, k1, c1, k2, c2, k3, c3, out,
    xc, xl, xr, x3, l1, l2, direct, turned, inside, w1, w2, w3, b1, b2, b3, bufs,
    load_sem, halo_send, halo_recv, send_sem, side_sem, recv_sem,
):
    i, j = lax.axis_index("row"), lax.axis_index("col")
    cx, cy, cz, core = i // 2, (j // 2) % 4, (i % 2) * 2 + j // 8, j % 2
    u1 = (cx // 2 + cz) % 2
    u2 = (cx + cy // 2) % 2
    u3 = (cy + cz // 2) % 2
    w = u1 * 4 + u2 * 2 + u3
    fixed = w == 0

    def chip(flips, c):
        x_ = flipped(cx, flips % 4)
        y_ = flipped(cy, (flips // 4) % 4)
        z_ = flipped(cz, (flips // 16) % 4)
        return (x_ * 2 + z_ // 2, (z_ % 2) * 8 + y_ * 2 + c)

    loads = [(x, xc.at[8:136]), (c1, b1), (c2, b2), (c3, b3)]
    for k, wide in ((k1, w1), (k2, w2)):
        loads.append((k, wide.at[0:1152, 0:128]))
        loads.append((k, wide.at[384:1536, 128:256]))
    loads.append((k3, w3.at[:, 0:128]))
    for a in range(3):
        for e in range(3):
            loads.append(
                (k3.at[pl.ds((e * 3 + a) * 128, 128)], w3.at[pl.ds((a * 3 + e) * 128, 128), 128:256])
            )
    loads = [pltpu.make_async_copy(s, d, load_sem.at[n]) for n, (s, d) in enumerate(loads)]
    for copy in loads:
        copy.start()

    barrier = pltpu.get_barrier_semaphore()
    out_codes = [pick(w, v) for v in OUT]
    in_codes = [pick(w, v) for v in INTO]

    def greet(device):
        pl.semaphore_signal(barrier, 1, device_id=device, device_id_type=MESH)

    def exists(di, dj):
        ok = None
        for ok_ in ([i + di >= 0, i + di < 8] if di else []) + ([j + dj >= 0, j + dj < 16] if dj else []):
            ok = ok_ if ok is None else both(ok, ok_)
        return ok

    expected = jnp.int32(0)
    for di in (-1, 0, 1):
        for dj in (-1, 0, 1):
            if di or dj:
                ok = exists(di, dj)
                expected = expected + jnp.where(ok, 1, 0)
                pl.when(ok)(lambda di=di, dj=dj: greet((i + di, j + dj)))

    @pl.when(fixed)
    def _():
        greet((i, j + 1 - 2 * core))

    straight = pick(w, STRAIGHT)
    long = straight >= 64

    @pl.when(long)
    def _():
        greet(chip(straight, 0))
        greet(chip(straight, 1))

    expected = expected + jnp.where(fixed, 1, 0) + jnp.where(long, 2, 0)
    for n in range(2 + SLOTS):
        came, goes = in_codes[n], out_codes[n]

        @pl.when(came >= 512)
        def _():
            if n < 2:
                greet(chip(came, 0))
                greet(chip(came, 1))
            else:
                greet(chip(came, core))

        expected = expected + jnp.where(goes >= 512, 1 + (goes // 64) % 2, 0)
    pl.semaphore_wait(barrier, expected)

    targets = {"c": xc, "l": xl, "r": xr}
    halo = []
    for n, (di, dj, rows, cols, name, into) in enumerate(HALO):
        copy = pltpu.make_async_remote_copy(
            x.at[rows, cols],
            targets[name].at[into],
            halo_send.at[n],
            halo_recv.at[n],
            device_id=(i + di, j + dj),
            device_id_type=MESH,
        )
        goes, comes = exists(di, dj), exists(-di, -dj)
        halo.append((copy, goes, comes))
        pl.when(goes)(copy.start)

        @pl.when(jnp.logical_not(comes))
        def _():
            ref = targets[name].at[into]
            ref[...] = jnp.zeros(ref.shape, BF16)

    for wide in (w1, w2):
        wide[1152:1536, 0:128] = jnp.zeros((384, 128), BF16)
        wide[0:384, 128:256] = jnp.zeros((384, 128), BF16)
    column = lax.broadcasted_iota(jnp.int32, (80, 128), 0) + (j * 64 - 8)
    inside[0] = jnp.zeros((80, 128), F32)
    inside[1] = jnp.where(both(column >= 0, column < 1024), 1.0, 0.0).astype(F32)

    def keep(row):
        at = i * 128 + row - 8
        return inside[jnp.where(both(at >= 0, at < 1024), 1, 0)]

    for copy in loads:
        copy.wait()

    def halo_wait(ns):
        for n in ns:
            copy, _, comes = halo[n]
            pl.when(comes)(copy.wait_recv)

    def spread(row):
        v = jnp.concatenate([xl[row].astype(F32), xc[row].astype(F32), xr[row].astype(F32)], axis=0)
        x3[row, :, 0:128] = pltpu.roll(v, 1, 0).astype(BF16)
        x3[row, :, 128:256] = v.astype(BF16)
        x3[row, :, 256:384] = pltpu.roll(v, 79, 0).astype(BF16)

    def pair_conv(ref, wide, bias, rows, d):
        lhs = jnp.concatenate(
            [jnp.concatenate([ref[r + (n - 1) * d] for n in range(4)], axis=-1) for r in rows], axis=0
        )
        total = jnp.dot(lhs, wide[...], preferred_element_type=F32)
        done = []
        for n, r in enumerate(rows):
            for m in range(2):
                v = total[n * 80 : n * 80 + 80, m * 128 : m * 128 + 128]
                done.append((r + m * d, jnp.maximum(v + bias[...], 0.0) * keep(r + m * d)))
        return done

    def near(base, count):
        for row, v in pair_conv(x3, w1, b1, [base + 2 * n for n in range(count // 2)], 1):
            l1[row, :, 0:128] = pltpu.roll(v, 2, 0).astype(BF16)
            l1[row, :, 128:256] = v.astype(BF16)
            l1[row, :, 256:384] = pltpu.roll(v, 78, 0).astype(BF16)

    def middle(base, count):
        rows = [base + 4 * n + s for n in range(count // 4) for s in range(2)]
        for row, v in pair_conv(l1, w2, b2, rows, 2):
            l2[row, :, 0:128] = pltpu.roll(v, 4, 0)[8:72].astype(BF16)
            l2[row, :, 128:256] = v[8:72].astype(BF16)
            l2[row, :, 256:384] = pltpu.roll(v, 76, 0)[8:72].astype(BF16)

    def far(t):
        base = t * ROWS
        lhs = jnp.concatenate(
            [jnp.concatenate([l2[base + 8 + r + 4 * a] for a in (-1, 0, 1)], axis=-1) for r in range(ROWS)], axis=0
        )
        total = jnp.dot(lhs, w3[...], preferred_element_type=F32)
        for r in range(ROWS):
            direct[base + r] = total[r * 64 : r * 64 + 64, 0:128] * 0.5 + b3[...]
            turned[pl.ds(r, 64, stride=ROWS), :] = total[r * 64 : r * 64 + 64, 128:256] * 0.5
        for path in range(2):
            v = turned[path * 32 * ROWS : (path + 1) * 32 * ROWS, :]
            bufs[7 + path, t] = v.reshape(32, ROWS, 128).astype(BF16)

    goes_on = [code >= 512 for code in out_codes]
    ends = [(code // 64) % 2 == 1 for code in out_codes]
    where = [chip(code, 0) for code in out_codes]
    slots = [
        jnp.where(end, core * 2 + (code // 128) % 4, 4 + (code // 128) % 4) for code, end in zip(out_codes, ends)
    ]

    target = chip(straight, 0)

    def hop(n, t, direct=None):
        row, col = where[n]
        end, slot = ends[n], slots[n]
        if direct is not None:
            row, col = jnp.where(direct, target[0], row), jnp.where(direct, target[1], col)
            end, slot = jnp.logical_or(direct, end), jnp.where(direct, core * 2, slot)
        return pltpu.make_async_remote_copy(
            bufs.at[7 + n if n < 2 else 2 + n, t],
            bufs.at[slot, t],
            send_sem.at[n, t],
            recv_sem.at[slot, t],
            device_id=(row, col + jnp.where(end, t // HALF, core)),
            device_id_type=MESH,
        )

    def across(n, t):
        return pltpu.make_async_remote_copy(
            bufs.at[7 + n, t],
            bufs.at[core * 2 + n, t],
            side_sem.at[n],
            recv_sem.at[core * 2 + n, t],
            device_id=(i, j + 1 - 2 * core),
            device_id_type=MESH,
        )

    def arrived(slot, t):
        here = bufs.at[slot, t]
        pltpu.make_async_copy(here, here, recv_sem.at[slot, t]).wait()

    def left(op, n):
        hop(op, lax.rem(n + 1, STEPS)).wait_send()

    def send(n):
        t = lax.rem(n + 1, STEPS)

        @pl.when(both(jnp.logical_not(fixed), n >= AHEAD))
        def _():
            for op in range(2):
                left(op, n - AHEAD)

        @pl.when(jnp.logical_not(fixed))
        def _():
            hop(0, t, both(long, n >= STEPS - DIRECT)).start()
            hop(1, t).start()

        @pl.when(both(fixed, t // HALF != core))
        def _():
            for n in range(2):
                across(n, t).start()

        @pl.when(both(fixed, t // HALF == core))
        def _():
            for n in range(2):
                own = core * 2 + n
                pltpu.make_async_copy(bufs.at[7 + n, t], bufs.at[own, t], recv_sem.at[own, t]).start()

    steps = [
        jnp.int32(STEPS - DIRECT) if s == 2 else jnp.where(ends[2 + s], STEPS, STEPS - DIRECT) for s in range(SLOTS)
    ]

    def relay(s, n):
        @pl.when(both(goes_on[2 + s], both(n >= LAG[s], n < steps[s] + LAG[s])))
        def _():
            t = lax.rem(n - LAG[s] + 1, STEPS)
            arrived(4 + s, t)
            pl.when(n >= LAG[s] + AHEAD)(lambda: left(2 + s, n - LAG[s] - AHEAD))
            hop(2 + s, t).start()

    def first(n, low, offset):
        return jnp.where(n >= STEPS - 1, low, (n + 1) * ROWS + offset)

    def feed(n):
        base = jnp.maximum(first(n, 1, 15), jnp.where(n < 0, 8, 0))
        for r in range(ROWS):
            spread(base + r)

    def one(n):
        near(first(n, 2, 14), ROWS)

    def two(n):
        middle(first(n, 4, 12), ROWS)

    halo_wait([0, 1])
    feed(jnp.int32(-2))

    def fill(n, carry):
        @pl.when(n == 0)
        def _():
            halo_wait([2, 3])

        one(n)
        feed(n + 1)
        pl.when(n >= -1)(lambda: two(n))
        return carry

    lax.fori_loop(-2, 1, fill, 0)

    def step(n, carry):
        for at, which in ((4, [4, 5]), (12, [9, 10, 11]), (13, [6, 7, 8])):
            pl.when(n == at)(lambda which=which: halo_wait(which))
        t = lax.rem(n + 1, STEPS)
        far(t)
        one(n + 1)
        feed(n + 2)
        send(n)
        relay(2, n)
        pl.when(n < STEPS - 1)(lambda: two(n + 1))
        relay(0, n)
        relay(1, n)
        return carry

    lax.fori_loop(0, STEPS, step, 0)

    def drain(d, carry):
        for s in range(SLOTS):
            relay(s, STEPS + d)

        @pl.when(d >= 1)
        def _():
            m = jnp.where(core == 0, lax.rem(d, HALF), d - 1)
            t = core * HALF + m
            cols = pl.ds(pl.multiple_of(m * ROWS, ROWS), ROWS)
            for slot in range(4):
                arrived(slot, t)
                rows = slice(slot * 32, slot * 32 + 32)
                out[rows, cols] = (direct[rows, cols] + bufs[slot, t].astype(F32)).astype(BF16)

        return carry

    lax.fori_loop(0, HALF + 1, drain, 0)

    for copy, goes, _ in halo:
        pl.when(goes)(copy.wait_send)
    for op in range(2 + SLOTS):

        @pl.when(goes_on[op])
        def _():
            for n in range(AHEAD):
                left(op, (STEPS if op < 2 else steps[op - 2]) - AHEAD + n)

    @pl.when(fixed)
    def _():
        for n in range(2):
            sent = bufs.at[7 + n, 0:HALF]
            pltpu.make_async_copy(sent, sent, side_sem.at[n]).wait()


def local(contact_map, kernel_near, offset_near, kernel_mid, offset_mid, kernel_far, offset_far):
    hbm, vmem = pl.BlockSpec(memory_space=pltpu.HBM), pl.BlockSpec(memory_space=pltpu.VMEM)
    args = [contact_map]
    for k, b in ((kernel_near, offset_near), (kernel_mid, offset_mid), (kernel_far, offset_far)):
        args += [k.reshape(9 * 128, 128), b.reshape(1, 128)]
    args = [pltpu.with_memory_space_constraint(v, pltpu.HBM) for v in args]
    dma = pltpu.SemaphoreType.DMA
    return pl.pallas_call(
        kernel,
        out_shape=jax.ShapeDtypeStruct((128, 64, 128), BF16),
        in_specs=[hbm] * 7,
        out_specs=vmem,
        scratch_shapes=[
            pltpu.VMEM((144, 64, 128), BF16),
            pltpu.VMEM((144, 8, 128), BF16),
            pltpu.VMEM((144, 8, 128), BF16),
            pltpu.VMEM((144, 80, 384), BF16),
            pltpu.VMEM((144, 80, 384), BF16),
            pltpu.VMEM((144, 64, 384), BF16),
            pltpu.VMEM((128, 64, 128), F32),
            pltpu.VMEM((65 * ROWS, 128), F32),
            pltpu.VMEM((2, 80, 128), F32),
            pltpu.VMEM((1536, 256), BF16),
            pltpu.VMEM((1536, 256), BF16),
            pltpu.VMEM((1152, 256), BF16),
            pltpu.VMEM((1, 128), F32),
            pltpu.VMEM((1, 128), F32),
            pltpu.VMEM((1, 128), F32),
            pltpu.VMEM((9, STEPS, 32, ROWS, 128), BF16),
            dma((18,)),
            dma((len(HALO),)),
            dma((len(HALO),)),
            dma((2 + SLOTS, STEPS)),
            dma((2,)),
            dma((7, STEPS)),
        ],
        compiler_params=pltpu.CompilerParams(
            collective_id=0, has_side_effects=True, vmem_limit_bytes=50 * 1024 * 1024
        ),
        name="trunk",
    )(*args)


def solution(mesh):
    in_specs = (P("row", "col", None), P(), P(), P(), P(), P(), P())
    return jax.shard_map(local, mesh=mesh, in_specs=in_specs, out_specs=P("row", "col", None), check_vma=False)
```

```python
import jax
import jax.numpy as jnp
from jax import lax
from jax.experimental import pallas as pl
from jax.experimental.pallas import tpu as pltpu
from jax.sharding import PartitionSpec as P

MESH = pl.DeviceIdType.MESH
F32, BF16 = jnp.float32, jnp.bfloat16

FLIPS = {
    "x0": ((1, 0, 0), 2),
    "x1": ((3, 0, 0), 6),
    "y0": ((0, 1, 0), 1),
    "y1": ((0, 3, 0), 3),
    "z0": ((0, 0, 1), 4),
    "z1": ((0, 0, 3), 5),
}
PATHS = {
    1: ("y0z1 z0", "z0z1 y0"),
    2: ("y1 x0y0", "y0y1 x0"),
    3: ("x0z1 y1z0", "z0z1 x0y1"),
    4: ("x1z0 x0", "x0x1z0"),
    5: ("x1z1 y0 x0", "x0y0z1 x1"),
    6: ("y1 y0z0 x1", "z0 x1y0y1"),
    7: ("x1y1z1", "y1z1 x1"),
}
STEPS = 16
ROWS = 8
LAG = (3, 3, 5)
AHEAD = 3
DIRECT = 1
SLOTS = len(LAG)
HALF = STEPS // 2


def segment(text):
    flips, change = [0, 0, 0], 0
    for at in range(0, len(text), 2):
        move, turn = FLIPS[text[at : at + 2]]
        flips = [a ^ b for a, b in zip(flips, move)]
        change ^= turn
    return tuple(flips), change


def plan():
    hops = []
    for start, paths in PATHS.items():
        for path, text in enumerate(paths):
            here, came = start, None
            for depth, part in enumerate(text.split()):
                flips, change = segment(part)
                hops.append([start, path, depth, here, flips, came])
                here, came = here ^ change, flips
            hops.append([start, path, depth + 1, here, None, came])
    relays = {w: [] for w in range(8)}
    for start, path, depth, here, flips, came in hops:
        if depth and flips is not None:
            relays[here].append((depth, start, path))
    slot = {}
    for w, held in relays.items():
        held.sort()
        taken = set()
        for depth, start, path in held:
            options = (2,) if depth == 2 else (0, 1, 2)
            at = [s for s in options if s not in taken][0]
            taken.add(at)
            slot[start, path, depth] = at
    out = [[0] * 8 for _ in range(2 + SLOTS)]
    into = [[0] * 8 for _ in range(2 + SLOTS)]
    code = lambda f: f[0] + 4 * f[1] + 16 * f[2]
    for start, path, depth, here, flips, came in hops:
        own = path if depth == 0 else None if flips is None else 2 + slot[start, path, depth]
        if flips is not None:
            after = slot.get((start, path, depth + 1))
            final = after is None
            out[own][here] = code(flips) + 64 * final + 128 * (path if final else after) + 512
        if came is not None:
            into[path if flips is None else own][here] = code(came) + 512
    return out, into


OUT, INTO = plan()
STRAIGHT = [0] * 8
for start, paths in PATHS.items():
    if len(paths[0].split()) == 3:
        flips, _ = segment(paths[0].replace(" ", ""))
        STRAIGHT[start] = flips[0] + 4 * flips[1] + 16 * flips[2] + 64


def pick(w, values):
    result = jnp.int32(values[0])
    for k in range(1, 8):
        result = jnp.where(w == k, jnp.int32(values[k]), result)
    return result


def both(a, b):
    return jnp.logical_and(a, b)


def flipped(value, by):
    return ((value // 2 + by // 2) % 2) * 2 + (value + by) % 2


ALL, LEFT, RIGHT = slice(0, 64), slice(0, 8), slice(56, 64)
HALO = []
for lo, hi in ((0, 24), (24, 48), (48, 128)):
    HALO.append((0, -1, slice(lo, hi), LEFT, "r", slice(8 + lo, 8 + hi)))
    HALO.append((0, 1, slice(lo, hi), RIGHT, "l", slice(8 + lo, 8 + hi)))
for di, src, dst in ((1, slice(121, 128), slice(1, 8)), (-1, slice(0, 7), slice(136, 143))):
    HALO.append((di, 0, src, ALL, "c", dst))
    HALO.append((di, -1, src, LEFT, "r", dst))
    HALO.append((di, 1, src, RIGHT, "l", dst))


def kernel(
    x, k1, c1, k2, c2, k3, c3, out,
    xc, xl, xr, x3, l1, l2, direct, turned, inside, w1, w2, w3, b1, b2, b3, bufs,
    load_sem, halo_send, halo_recv, send_sem, side_sem, recv_sem,
):
    i, j = lax.axis_index("row"), lax.axis_index("col")
    cx, cy, cz, core = i // 2, (j // 2) % 4, (i % 2) * 2 + j // 8, j % 2
    u1 = (cx // 2 + cz) % 2
    u2 = (cx + cy // 2) % 2
    u3 = (cy + cz // 2) % 2
    w = u1 * 4 + u2 * 2 + u3
    fixed = w == 0

    def chip(flips, c):
        x_ = flipped(cx, flips % 4)
        y_ = flipped(cy, (flips // 4) % 4)
        z_ = flipped(cz, (flips // 16) % 4)
        return (x_ * 2 + z_ // 2, (z_ % 2) * 8 + y_ * 2 + c)

    loads = [(x, xc.at[8:136]), (c1, b1), (c2, b2), (c3, b3)]
    for k, wide in ((k1, w1), (k2, w2)):
        loads.append((k, wide.at[0:1152, 0:128]))
        loads.append((k, wide.at[384:1536, 128:256]))
    loads.append((k3, w3.at[:, 0:128]))
    for a in range(3):
        for e in range(3):
            loads.append(
                (k3.at[pl.ds((e * 3 + a) * 128, 128)], w3.at[pl.ds((a * 3 + e) * 128, 128), 128:256])
            )
    loads = [pltpu.make_async_copy(s, d, load_sem.at[n]) for n, (s, d) in enumerate(loads)]
    for copy in loads:
        copy.start()

    barrier = pltpu.get_barrier_semaphore()
    out_codes = [pick(w, v) for v in OUT]
    in_codes = [pick(w, v) for v in INTO]

    def greet(device):
        pl.semaphore_signal(barrier, 1, device_id=device, device_id_type=MESH)

    def exists(di, dj):
        ok = None
        for ok_ in ([i + di >= 0, i + di < 8] if di else []) + ([j + dj >= 0, j + dj < 16] if dj else []):
            ok = ok_ if ok is None else both(ok, ok_)
        return ok

    expected = jnp.int32(0)
    for di in (-1, 0, 1):
        for dj in (-1, 0, 1):
            if di or dj:
                ok = exists(di, dj)
                expected = expected + jnp.where(ok, 1, 0)
                pl.when(ok)(lambda di=di, dj=dj: greet((i + di, j + dj)))

    @pl.when(fixed)
    def _():
        greet((i, j + 1 - 2 * core))

    straight = pick(w, STRAIGHT)
    long = straight >= 64

    @pl.when(long)
    def _():
        greet(chip(straight, 0))
        greet(chip(straight, 1))

    expected = expected + jnp.where(fixed, 1, 0) + jnp.where(long, 2, 0)
    for n in range(2 + SLOTS):
        came, goes = in_codes[n], out_codes[n]

        @pl.when(came >= 512)
        def _():
            if n < 2:
                greet(chip(came, 0))
                greet(chip(came, 1))
            else:
                greet(chip(came, core))

        expected = expected + jnp.where(goes >= 512, 1 + (goes // 64) % 2, 0)
    pl.semaphore_wait(barrier, expected)

    targets = {"c": xc, "l": xl, "r": xr}
    halo = []
    for n, (di, dj, rows, cols, name, into) in enumerate(HALO):
        copy = pltpu.make_async_remote_copy(
            x.at[rows, cols],
            targets[name].at[into],
            halo_send.at[n],
            halo_recv.at[n],
            device_id=(i + di, j + dj),
            device_id_type=MESH,
        )
        goes, comes = exists(di, dj), exists(-di, -dj)
        halo.append((copy, goes, comes))
        pl.when(goes)(copy.start)

        @pl.when(jnp.logical_not(comes))
        def _():
            ref = targets[name].at[into]
            ref[...] = jnp.zeros(ref.shape, BF16)

    for wide in (w1, w2):
        wide[1152:1536, 0:128] = jnp.zeros((384, 128), BF16)
        wide[0:384, 128:256] = jnp.zeros((384, 128), BF16)
    column = lax.broadcasted_iota(jnp.int32, (80, 128), 0) + (j * 64 - 8)
    inside[0] = jnp.zeros((80, 128), F32)
    inside[1] = jnp.where(both(column >= 0, column < 1024), 1.0, 0.0).astype(F32)

    def keep(row):
        at = i * 128 + row - 8
        return inside[jnp.where(both(at >= 0, at < 1024), 1, 0)]

    for copy in loads:
        copy.wait()

    def halo_wait(ns):
        for n in ns:
            copy, _, comes = halo[n]
            pl.when(comes)(copy.wait_recv)

    def spread(row):
        v = jnp.concatenate([xl[row].astype(F32), xc[row].astype(F32), xr[row].astype(F32)], axis=0)
        x3[row, :, 0:128] = pltpu.roll(v, 1, 0).astype(BF16)
        x3[row, :, 128:256] = v.astype(BF16)
        x3[row, :, 256:384] = pltpu.roll(v, 79, 0).astype(BF16)

    def pair_conv(ref, wide, bias, rows, d):
        lhs = jnp.concatenate(
            [jnp.concatenate([ref[r + (n - 1) * d] for n in range(4)], axis=-1) for r in rows], axis=0
        )
        total = jnp.dot(lhs, wide[...], preferred_element_type=F32)
        done = []
        for n, r in enumerate(rows):
            for m in range(2):
                v = total[n * 80 : n * 80 + 80, m * 128 : m * 128 + 128]
                done.append((r + m * d, jnp.maximum(v + bias[...], 0.0) * keep(r + m * d)))
        return done

    def near(base, count):
        for row, v in pair_conv(x3, w1, b1, [base + 2 * n for n in range(count // 2)], 1):
            l1[row, :, 0:128] = pltpu.roll(v, 2, 0).astype(BF16)
            l1[row, :, 128:256] = v.astype(BF16)
            l1[row, :, 256:384] = pltpu.roll(v, 78, 0).astype(BF16)

    def middle(base, count):
        rows = [base + 4 * n + s for n in range(count // 4) for s in range(2)]
        for row, v in pair_conv(l1, w2, b2, rows, 2):
            l2[row, :, 0:128] = pltpu.roll(v, 4, 0)[8:72].astype(BF16)
            l2[row, :, 128:256] = v[8:72].astype(BF16)
            l2[row, :, 256:384] = pltpu.roll(v, 76, 0)[8:72].astype(BF16)

    def far(t):
        base = t * ROWS
        lhs = jnp.concatenate(
            [jnp.concatenate([l2[base + 8 + r + 4 * a] for a in (-1, 0, 1)], axis=-1) for r in range(ROWS)], axis=0
        )
        total = jnp.dot(lhs, w3[...], preferred_element_type=F32)
        for r in range(ROWS):
            direct[base + r] = total[r * 64 : r * 64 + 64, 0:128] * 0.5 + b3[...]
            turned[pl.ds(r, 64, stride=ROWS), :] = total[r * 64 : r * 64 + 64, 128:256] * 0.5
        for path in range(2):
            v = turned[path * 32 * ROWS : (path + 1) * 32 * ROWS, :]
            bufs[7 + path, t] = v.reshape(32, ROWS, 128).astype(BF16)

    goes_on = [code >= 512 for code in out_codes]
    ends = [(code // 64) % 2 == 1 for code in out_codes]
    where = [chip(code, 0) for code in out_codes]
    slots = [
        jnp.where(end, core * 2 + (code // 128) % 4, 4 + (code // 128) % 4) for code, end in zip(out_codes, ends)
    ]

    target = chip(straight, 0)

    def hop(n, t, direct=None):
        row, col = where[n]
        end, slot = ends[n], slots[n]
        if direct is not None:
            row, col = jnp.where(direct, target[0], row), jnp.where(direct, target[1], col)
            end, slot = jnp.logical_or(direct, end), jnp.where(direct, core * 2, slot)
        return pltpu.make_async_remote_copy(
            bufs.at[7 + n if n < 2 else 2 + n, t],
            bufs.at[slot, t],
            send_sem.at[n, t],
            recv_sem.at[slot, t],
            device_id=(row, col + jnp.where(end, t // HALF, core)),
            device_id_type=MESH,
        )

    def across(n, t):
        return pltpu.make_async_remote_copy(
            bufs.at[7 + n, t],
            bufs.at[core * 2 + n, t],
            side_sem.at[n],
            recv_sem.at[core * 2 + n, t],
            device_id=(i, j + 1 - 2 * core),
            device_id_type=MESH,
        )

    def arrived(slot, t):
        here = bufs.at[slot, t]
        pltpu.make_async_copy(here, here, recv_sem.at[slot, t]).wait()

    def left(op, n):
        hop(op, lax.rem(n + 1, STEPS)).wait_send()

    def send(n):
        t = lax.rem(n + 1, STEPS)

        @pl.when(both(jnp.logical_not(fixed), n >= AHEAD))
        def _():
            for op in range(2):
                left(op, n - AHEAD)

        @pl.when(jnp.logical_not(fixed))
        def _():
            hop(0, t, both(long, n >= STEPS - DIRECT)).start()
            hop(1, t).start()

        @pl.when(both(fixed, t // HALF != core))
        def _():
            for n in range(2):
                across(n, t).start()

        @pl.when(both(fixed, t // HALF == core))
        def _():
            for n in range(2):
                own = core * 2 + n
                pltpu.make_async_copy(bufs.at[7 + n, t], bufs.at[own, t], recv_sem.at[own, t]).start()

    steps = [
        jnp.int32(STEPS - DIRECT) if s == 2 else jnp.where(ends[2 + s], STEPS, STEPS - DIRECT) for s in range(SLOTS)
    ]

    def relay(s, n):
        @pl.when(both(goes_on[2 + s], both(n >= LAG[s], n < steps[s] + LAG[s])))
        def _():
            t = lax.rem(n - LAG[s] + 1, STEPS)
            arrived(4 + s, t)
            pl.when(n >= LAG[s] + AHEAD)(lambda: left(2 + s, n - LAG[s] - AHEAD))
            hop(2 + s, t).start()

    def first(n, low, offset):
        return jnp.where(n >= STEPS - 1, low, (n + 1) * ROWS + offset)

    def feed(n):
        base = jnp.maximum(first(n, 1, 15), jnp.where(n < 0, 8, 0))
        for r in range(ROWS):
            spread(base + r)

    def one(n):
        near(first(n, 2, 14), ROWS)

    def two(n):
        middle(first(n, 4, 12), ROWS)

    halo_wait([0, 1])
    feed(jnp.int32(-2))

    def fill(n, carry):
        @pl.when(n == 0)
        def _():
            halo_wait([2, 3])

        one(n)
        feed(n + 1)
        pl.when(n >= -1)(lambda: two(n))
        return carry

    lax.fori_loop(-2, 1, fill, 0)

    def step(n, carry):
        for at, which in ((2, [4, 5]), (12, [9, 10, 11]), (13, [6, 7, 8])):
            pl.when(n == at)(lambda which=which: halo_wait(which))
        t = lax.rem(n + 1, STEPS)
        far(t)
        one(n + 1)
        feed(n + 2)
        send(n)
        pl.when(n < STEPS - 1)(lambda: two(n + 1))
        relay(2, n)
        relay(0, n)
        relay(1, n)
        return carry

    lax.fori_loop(0, STEPS, step, 0)

    def drain(d, carry):
        for s in range(SLOTS):
            relay(s, STEPS + d)

        @pl.when(d >= 1)
        def _():
            m = jnp.where(core == 0, lax.rem(d, HALF), d - 1)
            t = core * HALF + m
            cols = pl.ds(pl.multiple_of(m * ROWS, ROWS), ROWS)
            for slot in range(4):
                arrived(slot, t)
                rows = slice(slot * 32, slot * 32 + 32)
                out[rows, cols] = (direct[rows, cols] + bufs[slot, t].astype(F32)).astype(BF16)

        return carry

    lax.fori_loop(0, HALF + 1, drain, 0)

    for copy, goes, _ in halo:
        pl.when(goes)(copy.wait_send)
    for op in range(2 + SLOTS):

        @pl.when(goes_on[op])
        def _():
            for n in range(AHEAD):
                left(op, (STEPS if op < 2 else steps[op - 2]) - AHEAD + n)

    @pl.when(fixed)
    def _():
        for n in range(2):
            sent = bufs.at[7 + n, 0:HALF]
            pltpu.make_async_copy(sent, sent, side_sem.at[n]).wait()


def local(contact_map, kernel_near, offset_near, kernel_mid, offset_mid, kernel_far, offset_far):
    hbm, vmem = pl.BlockSpec(memory_space=pltpu.HBM), pl.BlockSpec(memory_space=pltpu.VMEM)
    args = [contact_map]
    for k, b in ((kernel_near, offset_near), (kernel_mid, offset_mid), (kernel_far, offset_far)):
        args += [k.reshape(9 * 128, 128), b.reshape(1, 128)]
    args = [pltpu.with_memory_space_constraint(v, pltpu.HBM) for v in args]
    dma = pltpu.SemaphoreType.DMA
    return pl.pallas_call(
        kernel,
        out_shape=jax.ShapeDtypeStruct((128, 64, 128), BF16),
        in_specs=[hbm] * 7,
        out_specs=vmem,
        scratch_shapes=[
            pltpu.VMEM((144, 64, 128), BF16),
            pltpu.VMEM((144, 8, 128), BF16),
            pltpu.VMEM((144, 8, 128), BF16),
            pltpu.VMEM((144, 80, 384), BF16),
            pltpu.VMEM((144, 80, 384), BF16),
            pltpu.VMEM((144, 64, 384), BF16),
            pltpu.VMEM((128, 64, 128), F32),
            pltpu.VMEM((65 * ROWS, 128), F32),
            pltpu.VMEM((2, 80, 128), F32),
            pltpu.VMEM((1536, 256), BF16),
            pltpu.VMEM((1536, 256), BF16),
            pltpu.VMEM((1152, 256), BF16),
            pltpu.VMEM((1, 128), F32),
            pltpu.VMEM((1, 128), F32),
            pltpu.VMEM((1, 128), F32),
            pltpu.VMEM((9, STEPS, 32, ROWS, 128), BF16),
            dma((18,)),
            dma((len(HALO),)),
            dma((len(HALO),)),
            dma((2 + SLOTS, STEPS)),
            dma((2,)),
            dma((7, STEPS)),
        ],
        compiler_params=pltpu.CompilerParams(
            collective_id=0, has_side_effects=True, vmem_limit_bytes=50 * 1024 * 1024
        ),
        name="trunk",
    )(*args)


def solution(mesh):
    in_specs = (P("row", "col", None), P(), P(), P(), P(), P(), P())
    return jax.shard_map(local, mesh=mesh, in_specs=in_specs, out_specs=P("row", "col", None), check_vma=False)
```
